512 devices in a mesh: seg: 32 (over x, z_hi, core), bond: 16 (over z_lo, y).
Axes of the slice: x: 4, y: 4, z: 16 (z_hi: 4, z_lo: 4; z = z_hi * 4 + z_lo), core: 2. Of those that a mesh axis runs over, the one named last changes fastest.
Arguments:
- left_env: bfloat16 [32, 128, 128, 128], P('seg', None, 'bond'), may hold values from -1 to 1, as said below
- right_env: bfloat16 [32, 128, 128, 128], P('seg', None, 'bond'), may hold values from -1 to 1, as said below
- mpo_site: bfloat16 [32, 128, 8, 8, 8], P('seg', 'bond'), may hold values from -1 to 1, as said below
- start_state: bfloat16 [32, 128, 8, 128], P('seg'), may hold values from -6 to 6
Outputs:
- new_state: bfloat16 [32, 128, 8, 128], P('seg')
- new_left: bfloat16 [32, 128, 128, 128], P('seg', None, 'bond')
- energy: float32 [32], P('seg')
- second_image: float32 [32, 128, 8, 128], P('seg', 'bond')
The draws below stay inside these ranges and needn't reach their ends.
Inputs may be any that keep to these rules, and one draw needn't show every extreme that they name: left_env[s, a, w, c] equals left_env[s, c, w, a]. right_env[s, b, w, c] equals right_env[s, c, w, b]. mpo_site[s, w, u, i, j] equals mpo_site[s, w, u, j, i].
All inputs are finite; a program needn't handle non-finite values.
Results may differ from the reference program's by a relative error of at most 0.01.
Values may be sent and summed in bfloat16 or wider, within the bound.
A program may use at most 64 MiB of HBM per device.

```python
import jax
import jax.numpy as jnp
from jax import lax

M = 128
W = 128
DL = 8
WB = 8
SEGS = 32
N_BOND = 16


def symmetric_env(key, spread):
    base = jax.random.normal(jax.random.fold_in(key, 11), (SEGS, M, W, M), jnp.float32) * spread
    sym = 0.5 * (base + jnp.transpose(base, (0, 3, 2, 1)))
    return jnp.clip(sym, -1.0, 1.0).astype(jnp.bfloat16)


def draw_left_env(key, part):
    return symmetric_env(jax.random.fold_in(key, 1), M ** (-0.5))


def draw_right_env(key, part):
    return symmetric_env(jax.random.fold_in(key, 2), (M * W) ** (-0.5))


def draw_mpo_site(key, part):
    spread = (WB * DL) ** (-0.5)
    base = jax.random.normal(jax.random.fold_in(key, 3), (SEGS, W, WB, DL, DL), jnp.float32) * spread
    sym = 0.5 * (base + jnp.transpose(base, (0, 1, 2, 4, 3)))
    return jnp.clip(sym, -1.0, 1.0).astype(jnp.bfloat16)


def levels(rng, shape, cuts, smallest, largest):
    def one(position, parts):
        steps = jax.random.uniform(jax.random.fold_in(jax.random.fold_in(rng, 6), position), (parts,), jnp.float32, smallest / len(cuts), largest / len(cuts))
        return jnp.repeat(jnp.exp(steps), shape[position] // parts).reshape((-1,) + (1,) * (len(shape) - position - 1))

    factor_of = one(*cuts[0])
    for cut in cuts[1:]:
        factor_of = factor_of * one(*cut)
    return factor_of


def normal_values(rng, shape, deviation, most, pieces=(), kind=jnp.bfloat16):
    array = deviation * jax.random.normal(rng, shape, jnp.float32)
    if pieces:
        array = array * levels(rng, shape, pieces, -0.22, 0.18)
    return jnp.clip(array, -most, most).astype(kind)


def setup_inputs(seed: int = 0) -> dict:
    arg_keys = jax.random.split(jax.random.key(seed), 5)
    return {
        "left_env": draw_left_env(jax.random.fold_in(arg_keys[4], 71), 0),
        "right_env": draw_right_env(jax.random.fold_in(arg_keys[4], 71), 0),
        "mpo_site": draw_mpo_site(jax.random.fold_in(arg_keys[4], 71), 0),
        "start_state": normal_values(arg_keys[3], (SEGS, M, DL, M), 1.0, 6.0, ((0, 32),)),
    }


epsilon = 1e-06

def couple_group(left_group, mpo_group, vector):
    mixed_terms = jnp.dot(left_group.reshape(M * WB, M), vector.reshape(M, DL * M), preferred_element_type=jnp.float32)
    mixed_terms = mixed_terms.astype(jnp.bfloat16).reshape(M, WB, DL, M)
    coupled = jnp.einsum('vust,avtb->asub', mpo_group.astype(jnp.float32), mixed_terms.astype(jnp.float32))
    return coupled.astype(jnp.bfloat16)

def apply_operator(left_block, mpo_block, right_block, vector):

    def one_group(running, group_index):
        left_group = lax.dynamic_slice_in_dim(left_block, group_index * WB, WB, 1)
        mpo_group = lax.dynamic_slice_in_dim(mpo_block, group_index * WB, WB, 0)
        right_group = lax.dynamic_slice_in_dim(right_block, group_index * WB, WB, 1)
        coupled = couple_group(left_group, mpo_group, vector)
        partial_value = lax.dot_general(coupled.reshape(M * DL, WB * M), right_group.reshape(M, WB * M), (((1,), (1,)), ((), ())), preferred_element_type=jnp.float32)
        return (running + partial_value.reshape(M, DL, M), None)
    running, _ = lax.scan(one_group, jnp.zeros((M, DL, M), jnp.float32), jnp.arange(N_BOND, dtype=jnp.int32))
    return running

def grow_left(left_block, mpo_block, new_state):

    def one_group(group_index):
        left_group = lax.dynamic_slice_in_dim(left_block, group_index * WB, WB, 1)
        mpo_group = lax.dynamic_slice_in_dim(mpo_block, group_index * WB, WB, 0)
        coupled = couple_group(left_group, mpo_group, new_state)
        grown = lax.dot_general(new_state.reshape(M * DL, M), coupled.reshape(M * DL, WB * M), (((0,), (0,)), ((), ())), preferred_element_type=jnp.float32)
        return grown.astype(jnp.bfloat16).reshape(M, WB, M)
    stacked = lax.map(one_group, jnp.arange(N_BOND, dtype=jnp.int32))
    return jnp.transpose(stacked, (1, 0, 2, 3)).reshape(M, W, M)

def one_segment(packed):
    left_block, right_block, mpo_block, start_block = packed
    begin_vec = start_block.astype(jnp.float32)
    first_basis = begin_vec / jnp.sqrt(jnp.mean(begin_vec * begin_vec) + epsilon)
    first_image = apply_operator(left_block, mpo_block, right_block, first_basis.astype(jnp.bfloat16))
    rayleigh = jnp.mean(first_basis * first_image)
    residual = first_image - rayleigh * first_basis
    residual_size = jnp.sqrt(jnp.mean(residual * residual) + epsilon)
    second_basis = residual / residual_size
    second_image = apply_operator(left_block, mpo_block, right_block, second_basis.astype(jnp.bfloat16))
    curvature = jnp.mean(second_basis * second_image)
    middle = 0.5 * (rayleigh + curvature)
    half_gap = 0.5 * (rayleigh - curvature)
    lowest = middle - jnp.sqrt(half_gap * half_gap + residual_size * residual_size)
    offset = lowest - rayleigh
    length_value = jnp.sqrt(residual_size * residual_size + offset * offset)
    new_state = ((residual_size * first_basis + offset * second_basis) / length_value).astype(jnp.bfloat16)
    new_left = grow_left(left_block, mpo_block, new_state)
    return (new_state, new_left, lowest.astype(jnp.float32), second_image)

def reference(left_env, right_env, mpo_site, start_state):
    right_next = jnp.roll(right_env, -1, axis=0)
    new_state, new_left, energy, second_image = lax.map(one_segment, (left_env, right_next, mpo_site, start_state))
    return (new_state, new_left, energy, second_image)
```

```python
import jax
import jax.numpy as jnp
from jax import lax
from jax.experimental import pallas as pl
from jax.experimental.pallas import tpu as pltpu
from jax.sharding import PartitionSpec as P

epsilon = 1e-06
MESH = pl.DeviceIdType.MESH
f32, bf16 = jnp.float32, jnp.bfloat16


def total(value):
    return jnp.sum(jnp.sum(value, axis=1, keepdims=True), axis=0, keepdims=True)


def kernel(segs, bonds, left_hbm, right_hbm, mpo_hbm, start_hbm,
           state_ref, grown_ref, energy_ref, image_ref,
           left, right, mpo, start, spread, wide, stacked, coupler,
           coupled_1, coupled_2, partial, start_t, resid_t,
           send_1, send_2, recv_1, recv_2, resid, scal_send, scal_recv,
           grown_11, grown_x, grown_22,
           local_sem, ring_sem, block_send, block_recv, scal_send_sem, scal_recv_sem):
    seg, me = lax.axis_index("seg"), lax.axis_index("bond")
    before, after = lax.rem(seg + segs - 1, segs), lax.rem(seg + 1, segs)
    rows = partial.shape[0] // bonds
    entries = partial.shape[0] * partial.shape[1]
    peers = [lax.rem(me + step, bonds) for step in range(1, bonds)]

    barrier = pltpu.get_barrier_semaphore()
    pl.semaphore_signal(barrier, inc=1, device_id=(before, me), device_id_type=MESH)
    pl.semaphore_signal(barrier, inc=1, device_id=(after, me), device_id_type=MESH)
    for peer in peers:
        pl.semaphore_signal(barrier, inc=1, device_id=(seg, peer), device_id_type=MESH)

    loads = [
        pltpu.make_async_copy(source, target, local_sem.at[place])
        for place, (source, target) in enumerate(((start_hbm, start), (left_hbm, left), (mpo_hbm, mpo)))
    ]
    for load in loads:
        load.start()
    pl.semaphore_wait(barrier, bonds + 1)

    ring = pltpu.make_async_remote_copy(
        src_ref=right_hbm, dst_ref=right, send_sem=ring_sem.at[0], recv_sem=ring_sem.at[1],
        device_id=(before, me), device_id_type=MESH)
    ring.start()

    def level_major(source):
        spread[...] = source[...].astype(f32)
        for t in range(8):
            wide[:, t * 128:(t + 1) * 128] = spread[pl.ds(t, 128, stride=8), :].astype(bf16)

    def couple(target):
        def step(i, carry):
            mixed = jnp.dot(left[pl.ds(i * 256, 256), :], wide[...], preferred_element_type=f32)
            shaped = jnp.stack([mixed[:, t * 128:(t + 1) * 128].reshape(32, 8, 128) for t in range(8)], axis=1)
            shaped = shaped.reshape(2048, 128).astype(bf16)
            for g in range(4):
                pair = jnp.concatenate(
                    [shaped[g * 512:g * 512 + 256], shaped[g * 512 + 256:g * 512 + 512]], axis=1)
                out = jnp.dot(coupler[...], pair, preferred_element_type=f32)
                for h in range(2):
                    half = out[:, h * 128:(h + 1) * 128].reshape(4, 8, 8, 128)
                    for u in range(8):
                        target[pl.ds(i * 256 + g * 64 + h * 32, 32), u * 128:(u + 1) * 128] = (
                            half[:, u].reshape(32, 128).astype(bf16))
            return carry
        lax.fori_loop(0, 4, step, 0)

    def image(source, vector, sent, scale):
        def step(i, carry):
            span = pl.ds(i * 256, 256)
            part = jnp.dot(source[span, :], stacked[...], preferred_element_type=f32)
            dots = jnp.sum((part * vector[span, :].astype(f32)).reshape(32, 8, 128), axis=0)
            if scale is not None:
                part = part * scale
            partial[span, :] = part
            sent[span, :] = part.astype(bf16)
            return carry + dots
        return total(lax.fori_loop(0, 4, step, jnp.zeros((8, 128), f32)))

    def grow(pairs, target):
        for u in range(0, 8, 2):
            lanes = slice(u * 128, (u + 2) * 128)
            value = None
            for transposed, source in pairs:
                term = jnp.dot(transposed[...], source[:, lanes], preferred_element_type=f32)
                value = term if value is None else value + term
            target[pl.ds(u, 128, stride=8), :] = value[:, :128]
            target[pl.ds(u + 1, 128, stride=8), :] = value[:, 128:]

    def scalar_round(phase, value):
        scal_send[phase] = jnp.broadcast_to(value, (8, 128))
        copies = []
        for step, peer in enumerate(peers):
            copies.append(pltpu.make_async_remote_copy(
                src_ref=scal_send.at[phase], dst_ref=scal_recv.at[phase, me],
                send_sem=scal_send_sem.at[phase, step], recv_sem=scal_recv_sem.at[phase, step],
                device_id=(seg, peer), device_id_type=MESH))
            copies[-1].start()
        scal_recv[phase, me] = scal_send[phase]
        return copies

    def scalar_sum(phase, copies):
        for copy in copies:
            copy.wait()
        return jnp.sum(scal_recv[phase], axis=0)[:1, :1]

    def scatter_round(phase, source, target):
        copies = []
        for step, peer in enumerate(peers):
            copies.append(pltpu.make_async_remote_copy(
                src_ref=source.at[pl.ds(pl.multiple_of(peer * rows, rows), rows), :], dst_ref=target.at[step],
                send_sem=block_send.at[phase, step], recv_sem=block_recv.at[phase, step],
                device_id=(seg, peer), device_id_type=MESH))
            copies[-1].start()
        return copies

    own = pl.ds(pl.multiple_of(me * rows, rows), rows)

    def scatter_sum(copies, target):
        value = partial[own, :]
        for step, copy in enumerate(copies):
            copy.wait()
            value = value + target[step].astype(f32)
        return value

    loads[0].wait()
    level_major(start)
    norm = total(jnp.sum((spread[...] * spread[...]).reshape(-1, 8, 128), axis=0))
    inverse = 1.0 / jnp.sqrt(norm / entries + epsilon)
    loads[2].wait()
    spot = lax.broadcasted_iota(jnp.int32, (8, 256), 0)
    lane = lax.broadcasted_iota(jnp.int32, (8, 256), 1)
    compact = jnp.zeros((64, 256), f32)
    for w in range(8):
        chosen = jnp.where(lax.rem(lane, 64) == spot * 8 + w, 1.0, 0.0).astype(f32)
        compact = compact + jnp.dot(
            mpo[w].astype(f32).reshape(64, 8), chosen, preferred_element_type=f32)
    tall = jnp.concatenate([compact] * 4, axis=0)
    row_group = lax.broadcasted_iota(jnp.int32, (256, 256), 0) // 64
    lane_group = lax.broadcasted_iota(jnp.int32, (256, 256), 1) // 64
    coupler[...] = jnp.where(row_group == lane_group, tall, 0.0).astype(bf16)
    loads[1].wait()
    couple(coupled_1)
    start_t[...] = jnp.transpose(start[...])

    ring.wait()
    spread[...] = right[...].astype(f32)
    for u in range(8):
        stacked[u * 128:(u + 1) * 128, :] = spread[pl.ds(u, 128, stride=8), :].astype(bf16)
    ray_copies = scalar_round(0, image(coupled_1, start, send_1, None))
    copies = scatter_round(0, send_1, recv_1)
    grow([(start_t, coupled_1)], grown_11)
    rayleigh = scalar_sum(0, ray_copies) * (inverse * inverse / entries)
    image_1 = scatter_sum(copies, recv_1)
    block = inverse * image_1 - (rayleigh * inverse) * start[own, :].astype(f32)
    resid[own, :] = block.astype(bf16)
    size_copies = scalar_round(1, total(block * block))
    copies = []
    for step, peer in enumerate(peers):
        copies.append(pltpu.make_async_remote_copy(
            src_ref=resid.at[own, :], dst_ref=resid.at[own, :],
            send_sem=block_send.at[1, step], recv_sem=block_recv.at[1, step],
            device_id=(seg, peer), device_id_type=MESH))
        copies[-1].start()
    for copy in copies:
        copy.wait()

    level_major(resid)
    couple(coupled_2)
    size = jnp.sqrt(scalar_sum(1, size_copies) / entries + epsilon)
    curve = image(coupled_2, resid, send_2, 1.0 / size)
    curve_copies = scalar_round(2, curve)
    copies = scatter_round(2, send_2, recv_2)
    resid_t[...] = jnp.transpose(resid[...])
    grow([(start_t, coupled_2), (resid_t, coupled_1)], grown_x)
    grow([(resid_t, coupled_2)], grown_22)
    curvature = scalar_sum(2, curve_copies) / (size * size * entries)
    middle = 0.5 * (rayleigh + curvature)
    half_gap = 0.5 * (rayleigh - curvature)
    lowest = middle - jnp.sqrt(half_gap * half_gap + size * size)
    offset = lowest - rayleigh
    length = jnp.sqrt(size * size + offset * offset)
    first = size / length * inverse
    second = offset / length / size
    energy_ref[0] = lowest[0, 0]
    state_ref[...] = (first * start[...].astype(f32) + second * resid[...].astype(f32)).astype(bf16)
    grown_ref[...] = (first * first * grown_11[...] + first * second * grown_x[...]
                      + second * second * grown_22[...]).astype(bf16)
    image_ref[...] = scatter_sum(copies, recv_2)


def solution(mesh):
    segs, bonds = mesh.shape["seg"], mesh.shape["bond"]

    def body(left_env, right_env, mpo_site, start_state):
        big, half = (1024, 128), (1024 // bonds, 128)
        anywhere = pl.BlockSpec(memory_space=pl.ANY)
        vmem = pl.BlockSpec(memory_space=pltpu.VMEM)
        state, grown, energy, image = pl.pallas_call(
            lambda *refs: kernel(segs, bonds, *refs),
            out_shape=(
                jax.ShapeDtypeStruct(big, bf16),
                jax.ShapeDtypeStruct(big, bf16),
                jax.ShapeDtypeStruct((1,), f32),
                jax.ShapeDtypeStruct(half, f32),
            ),
            in_specs=[anywhere] * 4,
            out_specs=(vmem, vmem, pl.BlockSpec(memory_space=pltpu.SMEM), vmem),
            scratch_shapes=[
                pltpu.VMEM(big, bf16),
                pltpu.VMEM(big, bf16),
                pltpu.VMEM((8, 8, 8, 8), bf16),
                pltpu.VMEM(big, bf16),
                pltpu.VMEM(big, f32),
                pltpu.VMEM((128, 1024), bf16),
                pltpu.VMEM(big, bf16),
                pltpu.VMEM((256, 256), bf16),
                pltpu.VMEM((1024, 1024), bf16),
                pltpu.VMEM((1024, 1024), bf16),
                pltpu.VMEM(big, f32),
                pltpu.VMEM((128, 1024), bf16),
                pltpu.VMEM((128, 1024), bf16),
                pltpu.VMEM(big, bf16),
                pltpu.VMEM(big, bf16),
                pltpu.VMEM((bonds - 1,) + half, bf16),
                pltpu.VMEM((bonds - 1,) + half, bf16),
                pltpu.VMEM(big, bf16),
                pltpu.VMEM((3, 8, 128), f32),
                pltpu.VMEM((3, bonds, 8, 128), f32),
                pltpu.VMEM(big, f32),
                pltpu.VMEM(big, f32),
                pltpu.VMEM(big, f32),
                pltpu.SemaphoreType.DMA((3,)),
                pltpu.SemaphoreType.DMA((2,)),
                pltpu.SemaphoreType.DMA((3, bonds - 1)),
                pltpu.SemaphoreType.DMA((3, bonds - 1)),
                pltpu.SemaphoreType.DMA((3, bonds - 1)),
                pltpu.SemaphoreType.DMA((3, bonds - 1)),
            ],
            compiler_params=pltpu.CompilerParams(
                collective_id=0, has_side_effects=True, vmem_limit_bytes=60 * 1024 * 1024),
            name="ritz_step",
        )(left_env.reshape(big), right_env.reshape(big), mpo_site[0], start_state.reshape(big))
        return (
            state.reshape(1, 128, 8, 128),
            grown.reshape(1, 128, 8, 128),
            energy,
            image.reshape(1, 1024 // bonds // 8, 8, 128),
        )

    in_specs = (
        P("seg", None, "bond", None),
        P("seg", None, "bond", None),
        P("seg", "bond", None, None, None),
        P("seg", None, None, None),
    )
    out_specs = (
        P("seg", None, None, None),
        P("seg", None, "bond", None),
        P("seg"),
        P("seg", "bond", None, None),
    )
    return jax.shard_map(body, mesh=mesh, in_specs=in_specs, out_specs=out_specs, check_vma=False)
```

```python
import jax
import jax.numpy as jnp
from jax import lax
from jax.experimental import pallas as pl
from jax.experimental.pallas import tpu as pltpu
from jax.sharding import PartitionSpec as P

epsilon = 1e-06
MESH = pl.DeviceIdType.MESH
f32, bf16 = jnp.float32, jnp.bfloat16
ROW, SIDE = 4, 4
CHUNKS = 4


def total(value):
    return jnp.sum(jnp.sum(value, axis=1, keepdims=True), axis=0, keepdims=True)


def kernel(segs, bonds, left_hbm, right_hbm, mpo_hbm, start_hbm,
           state_ref, grown_ref, energy_ref, image_ref,
           left, right, mpo, start, spread, wide, stacked, coupler, pack_send, pack_recv, edge_send, edge_recv,
           coupled_1, coupled_2, partial, start_t, resid_t,
           send_1, send_2, recv_1, recv_2, resid, scal_send, scal_recv,
           grown_11, grown_x, grown_22,
           local_sem, ring_send, ring_recv, block_send, block_recv, scal_send_sem, scal_recv_sem):
    seg, me = lax.axis_index("seg"), lax.axis_index("bond")
    before, after = lax.rem(seg + segs - 1, segs), lax.rem(seg + 1, segs)
    rows = partial.shape[0] // bonds
    entries = partial.shape[0] * partial.shape[1]
    row, place = me // SIDE, lax.rem(me, SIDE)
    row_order = [3 - row, lax.rem(row + 2, ROW), row + 1 - 2 * lax.rem(row, 2), row]
    peers = []
    for k, other in enumerate(row_order):
        for j in (2, 1, 3, 0):
            if k < 3 or j:
                peers.append(other * SIDE + lax.rem(place + j, SIDE))
    by_row = [range(0, 4), range(4, 8), range(8, 12), range(12, 15)]

    barrier = pltpu.get_barrier_semaphore()
    pl.semaphore_signal(barrier, inc=1, device_id=(before, me), device_id_type=MESH)
    pl.semaphore_signal(barrier, inc=1, device_id=(after, me), device_id_type=MESH)
    for peer in peers:
        pl.semaphore_signal(barrier, inc=1, device_id=(seg, peer), device_id_type=MESH)

    loads = [
        pltpu.make_async_copy(source, target, local_sem.at[spot])
        for spot, (source, target) in enumerate(
            ((right_hbm, right), (start_hbm, start), (left_hbm, left), (mpo_hbm, mpo)))
    ]
    for load in loads:
        load.start()

    up = lax.broadcasted_iota(jnp.int32, (64, 128), 0)
    lane = lax.broadcasted_iota(jnp.int32, (64, 128), 1)
    keep = jnp.where(lane < 64, jnp.where(lane <= up, 1, 0), jnp.where(lane - 64 > up, 1, 0)) == 1
    near, far = lane == up, lane == up + 64
    loads[0].wait()
    spread[...] = right[...].astype(f32)
    for u in range(8):
        low = spread[pl.ds(u, 64, stride=8), :]
        high = spread[pl.ds(512 + u, 64, stride=8), :]
        pack_send[u] = jnp.where(keep, low, high).astype(bf16)
        edge_send[u:u + 1, :] = jnp.sum(
            jnp.where(far, low, 0.0) + jnp.where(near, high, 0.0), axis=0, keepdims=True)
    pl.semaphore_wait(barrier, bonds + 1)

    share = 8 // CHUNKS
    ring = [pltpu.make_async_remote_copy(
        src_ref=edge_send, dst_ref=edge_recv, send_sem=ring_send.at[CHUNKS], recv_sem=ring_recv.at[CHUNKS],
        device_id=(before, me), device_id_type=MESH)]
    for c in range(CHUNKS):
        part = pl.ds(c * share, share)
        ring.append(pltpu.make_async_remote_copy(
            src_ref=pack_send.at[part], dst_ref=pack_recv.at[part],
            send_sem=ring_send.at[c], recv_sem=ring_recv.at[c],
            device_id=(before, me), device_id_type=MESH))
    for copy in ring:
        copy.start()

    def unpack(u):
        half = pack_recv[u].astype(f32)
        turned = jnp.transpose(jnp.concatenate([half, half], axis=0))
        edge = jnp.broadcast_to(edge_recv[u:u + 1, :], (64, 128))
        top = jnp.where(far, edge, jnp.where(keep, half, turned[:64]))
        low = jnp.where(near, edge, jnp.where(keep, turned[64:], half))
        stacked[u * 128:u * 128 + 64, :] = top.astype(bf16)
        stacked[u * 128 + 64:u * 128 + 128, :] = low.astype(bf16)

    def couple(target):
        def step(i, carry):
            mixed = jnp.dot(left[pl.ds(i * 256, 256), :], wide[...], preferred_element_type=f32)
            shaped = jnp.stack([mixed[:, t * 128:(t + 1) * 128].reshape(32, 8, 128) for t in range(8)], axis=1)
            shaped = shaped.reshape(2048, 128).astype(bf16)
            for g in range(4):
                pair = jnp.concatenate(
                    [shaped[g * 512:g * 512 + 256], shaped[g * 512 + 256:g * 512 + 512]], axis=1)
                out = jnp.dot(coupler[...], pair, preferred_element_type=f32)
                for h in range(2):
                    half = out[:, h * 128:(h + 1) * 128].reshape(4, 8, 8, 128)
                    for u in range(8):
                        target[pl.ds(i * 256 + g * 64 + h * 32, 32), u * 128:(u + 1) * 128] = (
                            half[:, u].reshape(32, 128).astype(bf16))
            return carry
        lax.fori_loop(0, 4, step, 0)

    def scatter_copy(phase, step, source, target):
        peer = peers[step]
        return pltpu.make_async_remote_copy(
            src_ref=source.at[pl.ds(pl.multiple_of(peer * rows, rows), rows), :], dst_ref=target.at[step],
            send_sem=block_send.at[phase, step], recv_sem=block_recv.at[phase, step],
            device_id=(seg, peer), device_id_type=MESH)

    def image(source, vector, sent, target, phase, scale, first, more):
        lanes = slice(first, 1024)
        dots = jnp.zeros((8, 128), f32)
        copies = []
        for k in range(4):
            span = pl.ds(pl.multiple_of(row_order[k] * 256, 256), 256)
            part = jnp.dot(source[span, lanes], stacked[lanes, :], preferred_element_type=f32)
            if more:
                part = part + partial[span, :]
            dots = dots + jnp.sum((part * vector[span, :].astype(f32)).reshape(32, 8, 128), axis=0)
            if scale is not None:
                part = part * scale
            partial[span, :] = part
            sent[span, :] = part.astype(bf16)
            for step in by_row[k]:
                copies.append(scatter_copy(phase, step, sent, target))
                copies[-1].start()
        return total(dots), copies

    def grow(pairs, target):
        for u in range(0, 8, 2):
            lanes = slice(u * 128, (u + 2) * 128)
            value = None
            for transposed, source in pairs:
                term = jnp.dot(transposed[...], source[:, lanes], preferred_element_type=f32)
                value = term if value is None else value + term
            target[pl.ds(u, 128, stride=8), :] = value[:, :128]
            target[pl.ds(u + 1, 128, stride=8), :] = value[:, 128:]

    def scalar_round(phase, value):
        scal_send[phase] = jnp.broadcast_to(value, (8, 128))
        copies = []
        for step, peer in enumerate(peers):
            copies.append(pltpu.make_async_remote_copy(
                src_ref=scal_send.at[phase], dst_ref=scal_recv.at[phase, me],
                send_sem=scal_send_sem.at[phase, step], recv_sem=scal_recv_sem.at[phase, step],
                device_id=(seg, peer), device_id_type=MESH))
            copies[-1].start()
        scal_recv[phase, me] = scal_send[phase]
        return copies

    def scalar_sum(phase, copies):
        for copy in copies:
            copy.wait()
        return jnp.sum(scal_recv[phase], axis=0)[:1, :1]

    own = pl.ds(pl.multiple_of(me * rows, rows), rows)

    def scatter_sum(copies, target):
        value = partial[own, :]
        for step in reversed(range(len(copies))):
            copies[step].wait()
            value = value + target[step].astype(f32)
        return value

    loads[1].wait()
    spread[...] = start[...].astype(f32)
    for t in range(8):
        wide[:, t * 128:(t + 1) * 128] = spread[pl.ds(t, 128, stride=8), :].astype(bf16)
    norm = total(jnp.sum((spread[...] * spread[...]).reshape(-1, 8, 128), axis=0))
    inverse = 1.0 / jnp.sqrt(norm / entries + epsilon)
    loads[3].wait()
    spot = lax.broadcasted_iota(jnp.int32, (8, 256), 0)
    wide_lane = lax.broadcasted_iota(jnp.int32, (8, 256), 1)
    compact = jnp.zeros((64, 256), f32)
    for w in range(8):
        chosen = jnp.where(lax.rem(wide_lane, 64) == spot * 8 + w, 1.0, 0.0).astype(f32)
        compact = compact + jnp.dot(
            mpo[w].astype(f32).reshape(64, 8), chosen, preferred_element_type=f32)
    tall = jnp.concatenate([compact] * 4, axis=0)
    row_group = lax.broadcasted_iota(jnp.int32, (256, 256), 0) // 64
    lane_group = lax.broadcasted_iota(jnp.int32, (256, 256), 1) // 64
    coupler[...] = jnp.where(row_group == lane_group, tall, 0.0).astype(bf16)
    loads[2].wait()
    couple(coupled_1)
    start_t[...] = jnp.transpose(start[...])

    ring[0].wait_recv()
    for c in range(CHUNKS):
        ring[1 + c].wait_recv()
        for u in range(c * share, (c + 1) * share):
            unpack(u)
        if c < CHUNKS - 1:
            def add(i, carry, c=c):
                span, lanes = pl.ds(i * 256, 256), slice(c * share * 128, (c + 1) * share * 128)
                part = jnp.dot(coupled_1[span, lanes], stacked[lanes, :], preferred_element_type=f32)
                partial[span, :] = part if c == 0 else partial[span, :] + part
                return carry
            lax.fori_loop(0, 4, add, 0)
    ray, copies = image(coupled_1, start, send_1, recv_1, 0, None, (CHUNKS - 1) * share * 128, True)
    ray_copies = scalar_round(0, ray)
    grow([(start_t, coupled_1)], grown_11)
    rayleigh = scalar_sum(0, ray_copies) * (inverse * inverse / entries)
    image_1 = scatter_sum(copies, recv_1)
    block = inverse * image_1 - (rayleigh * inverse) * start[own, :].astype(f32)
    resid[own, :] = block.astype(bf16)
    copies = []
    for step, peer in enumerate(peers):
        copies.append(pltpu.make_async_remote_copy(
            src_ref=resid.at[own, :], dst_ref=resid.at[own, :],
            send_sem=block_send.at[1, step], recv_sem=block_recv.at[1, step],
            device_id=(seg, peer), device_id_type=MESH))
        copies[-1].start()
    size_copies = scalar_round(1, total(block * block))

    for k in (3, 2, 1, 0):
        for step in by_row[k]:
            copies[step].wait()
        span = pl.ds(pl.multiple_of(row_order[k] * 256, 256), 256)
        spread[span, :] = resid[span, :].astype(f32)
        for t in range(8):
            wide[pl.ds(pl.multiple_of(row_order[k] * 32, 32), 32), t * 128:(t + 1) * 128] = (
                spread[pl.ds(row_order[k] * 256 + t, 32, stride=8), :].astype(bf16))
    couple(coupled_2)
    size = jnp.sqrt(scalar_sum(1, size_copies) / entries + epsilon)
    curve, copies = image(coupled_2, resid, send_2, recv_2, 2, 1.0 / size, 0, False)
    curve_copies = scalar_round(2, curve)
    resid_t[...] = jnp.transpose(resid[...])
    grow([(start_t, coupled_2), (resid_t, coupled_1)], grown_x)
    grow([(resid_t, coupled_2)], grown_22)
    curvature = scalar_sum(2, curve_copies) / (size * size * entries)
    middle = 0.5 * (rayleigh + curvature)
    half_gap = 0.5 * (rayleigh - curvature)
    lowest = middle - jnp.sqrt(half_gap * half_gap + size * size)
    offset = lowest - rayleigh
    length = jnp.sqrt(size * size + offset * offset)
    first = size / length * inverse
    second = offset / length / size
    energy_ref[...] = jnp.broadcast_to(lowest, (8, 128))
    state_ref[...] = (first * start[...].astype(f32) + second * resid[...].astype(f32)).astype(bf16)
    grown_ref[...] = (first * first * grown_11[...] + first * second * grown_x[...]
                      + second * second * grown_22[...]).astype(bf16)
    for copy in ring:
        copy.wait_send()
    image_ref[...] = scatter_sum(copies, recv_2)


def write_out(state, grown, energy, image, state_out, grown_out, energy_out, image_out, sems):
    copies = [
        pltpu.make_async_copy(source, target, sems.at[spot])
        for spot, (source, target) in enumerate(((state, state_out), (grown, grown_out), (image, image_out)))
    ]
    for copy in copies:
        copy.start()
    energy_out[0] = energy[0, 0]
    for copy in copies:
        copy.wait()


def solution(mesh):
    segs, bonds = mesh.shape["seg"], mesh.shape["bond"]

    def body(left_env, right_env, mpo_site, start_state):
        big, half = (1024, 128), (1024 // bonds, 128)
        anywhere = pl.BlockSpec(memory_space=pl.ANY)
        vmem = pl.BlockSpec(memory_space=pltpu.VMEM)
        results = pl.pallas_call(
            lambda *refs: kernel(segs, bonds, *refs),
            out_shape=(pltpu.VMEM(big, bf16), pltpu.VMEM(big, bf16), pltpu.VMEM((8, 128), f32), pltpu.VMEM(half, f32)),
            in_specs=[pl.BlockSpec(memory_space=pltpu.HBM)] * 4,
            out_specs=(vmem,) * 4,
            scratch_shapes=[
                pltpu.VMEM(big, bf16),
                pltpu.VMEM(big, bf16),
                pltpu.VMEM((8, 8, 8, 8), bf16),
                pltpu.VMEM(big, bf16),
                pltpu.VMEM(big, f32),
                pltpu.VMEM((128, 1024), bf16),
                pltpu.VMEM(big, bf16),
                pltpu.VMEM((256, 256), bf16),
                pltpu.VMEM((8, 64, 128), bf16),
                pltpu.VMEM((8, 64, 128), bf16),
                pltpu.VMEM((8, 128), f32),
                pltpu.VMEM((8, 128), f32),
                pltpu.VMEM((1024, 1024), bf16),
                pltpu.VMEM((1024, 1024), bf16),
                pltpu.VMEM(big, f32),
                pltpu.VMEM((128, 1024), bf16),
                pltpu.VMEM((128, 1024), bf16),
                pltpu.VMEM(big, bf16),
                pltpu.VMEM(big, bf16),
                pltpu.VMEM((bonds - 1,) + half, bf16),
                pltpu.VMEM((bonds - 1,) + half, bf16),
                pltpu.VMEM(big, bf16),
                pltpu.VMEM((3, 8, 128), f32),
                pltpu.VMEM((3, bonds, 8, 128), f32),
                pltpu.VMEM(big, f32),
                pltpu.VMEM(big, f32),
                pltpu.VMEM(big, f32),
                pltpu.SemaphoreType.DMA((4,)),
                pltpu.SemaphoreType.DMA((CHUNKS + 1,)),
                pltpu.SemaphoreType.DMA((CHUNKS + 1,)),
                pltpu.SemaphoreType.DMA((3, bonds - 1)),
                pltpu.SemaphoreType.DMA((3, bonds - 1)),
                pltpu.SemaphoreType.DMA((3, bonds - 1)),
                pltpu.SemaphoreType.DMA((3, bonds - 1)),
            ],
            compiler_params=pltpu.CompilerParams(
                collective_id=0, has_side_effects=True, vmem_limit_bytes=32 * 1024 * 1024),
            name="ritz_step",
        )(*(pltpu.with_memory_space_constraint(x, pltpu.HBM) for x in (
            left_env.reshape(big), right_env.reshape(big), mpo_site[0], start_state.reshape(big))))
        state, grown, energy, image = pl.pallas_call(
            write_out,
            out_shape=(
                jax.ShapeDtypeStruct(big, bf16),
                jax.ShapeDtypeStruct(big, bf16),
                jax.ShapeDtypeStruct((1,), f32),
                jax.ShapeDtypeStruct(half, f32),
            ),
            in_specs=[vmem] * 4,
            out_specs=(anywhere, anywhere, pl.BlockSpec(memory_space=pltpu.SMEM), anywhere),
            scratch_shapes=[pltpu.SemaphoreType.DMA((3,))],
            compiler_params=pltpu.CompilerParams(vmem_limit_bytes=8 * 1024 * 1024),
            name="write_out",
        )(*results)
        return (
            state.reshape(1, 128, 8, 128),
            grown.reshape(1, 128, 8, 128),
            energy,
            image.reshape(1, 1024 // bonds // 8, 8, 128),
        )

    in_specs = (
        P("seg", None, "bond", None),
        P("seg", None, "bond", None),
        P("seg", "bond", None, None, None),
        P("seg", None, None, None),
    )
    out_specs = (
        P("seg", None, None, None),
        P("seg", None, "bond", None),
        P("seg"),
        P("seg", "bond", None, None),
    )
    return jax.shard_map(body, mesh=mesh, in_specs=in_specs, out_specs=out_specs, check_vma=False)
```

```python
import jax
import jax.numpy as jnp
from jax import lax
from jax.experimental import pallas as pl
from jax.experimental.pallas import tpu as pltpu
from jax.sharding import PartitionSpec as P

epsilon = 1e-06
MESH = pl.DeviceIdType.MESH
f32, bf16 = jnp.float32, jnp.bfloat16
ROW, SIDE = 4, 4
CHUNKS = 4


def total(value):
    return jnp.sum(jnp.sum(value, axis=1, keepdims=True), axis=0, keepdims=True)


def kernel(segs, bonds, left_hbm, right_hbm, mpo_hbm, start_hbm,
           state_ref, grown_ref, energy_ref, image_ref,
           left, right, mpo, start, spread, wide, stacked, coupler, pack_send, pack_recv, edge_send, edge_recv,
           coupled_1, coupled_2, partial, start_t, resid_t,
           send_1, send_2, side_1, side_2, sums_1, sums_2, recv_1, recv_2, resid, scal_send, scal_recv,
           grown_11, grown_x, grown_22,
           ready, distant, local_sem, ring_send, ring_recv, block_send, block_recv, scal_send_sem, scal_recv_sem):
    seg, me = lax.axis_index("seg"), lax.axis_index("bond")
    before, after = lax.rem(seg + segs - 1, segs), lax.rem(seg + 1, segs)
    rows = partial.shape[0] // bonds
    entries = partial.shape[0] * partial.shape[1]
    row, place = me // SIDE, lax.rem(me, SIDE)
    row_order = [3 - row, lax.rem(row + 2, ROW), row + 1 - 2 * lax.rem(row, 2), row]
    peers = []
    for k, other in enumerate(row_order):
        for j in (2, 1, 3, 0):
            if k < 3 or j:
                peers.append(other * SIDE + lax.rem(place + j, SIDE))
    pending = []

    early, late = lax.rem(seg, 8) == 0, lax.rem(seg, 8) == 7
    beside = [row * SIDE + lax.rem(place + j, SIDE) for j in range(1, SIDE)]
    barrier = pltpu.get_barrier_semaphore()

    def enter(device, semaphore=barrier):
        pl.semaphore_signal(semaphore, inc=1, device_id=device, device_id_type=MESH)

    for peer in beside:
        enter((seg, peer))
    pl.when(jnp.logical_not(late))(lambda: enter((after, me)))
    pl.when(early)(lambda: enter((before, me)))
    for other in row_order[:3]:
        @pl.when(other > row)
        def _(other=other):
            for j in range(SIDE):
                enter((seg, other * SIDE + lax.rem(place + j, SIDE)))

    loads = [
        pltpu.make_async_copy(source, target, local_sem.at[spot])
        for spot, (source, target) in enumerate(
            ((right_hbm, right), (start_hbm, start), (left_hbm, left), (mpo_hbm, mpo)))
    ]
    for load in loads:
        load.start()

    up = lax.broadcasted_iota(jnp.int32, (64, 128), 0)
    lane = lax.broadcasted_iota(jnp.int32, (64, 128), 1)
    keep = jnp.where(lane < 64, jnp.where(lane <= up, 1, 0), jnp.where(lane - 64 > up, 1, 0)) == 1
    near, far = lane == up, lane == up + 64
    loads[0].wait()
    spread[...] = right[...].astype(f32)
    for u in range(8):
        low = spread[pl.ds(u, 64, stride=8), :]
        high = spread[pl.ds(512 + u, 64, stride=8), :]
        pack_send[u] = jnp.where(keep, low, high).astype(bf16)
        edge_send[u:u + 1, :] = jnp.sum(
            jnp.where(far, low, 0.0) + jnp.where(near, high, 0.0), axis=0, keepdims=True)
    pl.semaphore_wait(barrier, SIDE * row + SIDE - jnp.where(early, 1, 0) + jnp.where(late, 1, 0))
    for other in row_order[:3]:
        @pl.when(other < row)
        def _(other=other):
            for j in range(SIDE):
                enter((seg, other * SIDE + lax.rem(place + j, SIDE)), ready)
    pl.when(late)(lambda: enter((after, me), distant))

    share = 8 // CHUNKS
    ring = [pltpu.make_async_remote_copy(
        src_ref=edge_send, dst_ref=edge_recv, send_sem=ring_send.at[CHUNKS], recv_sem=ring_recv.at[CHUNKS],
        device_id=(before, me), device_id_type=MESH)]
    for c in range(CHUNKS):
        part = pl.ds(c * share, share)
        ring.append(pltpu.make_async_remote_copy(
            src_ref=pack_send.at[part], dst_ref=pack_recv.at[part],
            send_sem=ring_send.at[c], recv_sem=ring_recv.at[c],
            device_id=(before, me), device_id_type=MESH))

    @pl.when(jnp.logical_not(early))
    def _():
        for copy in ring:
            copy.start()

    def unpack(u):
        half = pack_recv[u].astype(f32)
        turned = jnp.transpose(jnp.concatenate([half, half], axis=0))
        edge = jnp.broadcast_to(edge_recv[u:u + 1, :], (64, 128))
        top = jnp.where(far, edge, jnp.where(keep, half, turned[:64]))
        low = jnp.where(near, edge, jnp.where(keep, turned[64:], half))
        stacked[u * 128:u * 128 + 64, :] = top.astype(bf16)
        stacked[u * 128 + 64:u * 128 + 128, :] = low.astype(bf16)

    def couple(target):
        def step(i, carry):
            mixed = jnp.dot(left[pl.ds(i * 256, 256), :], wide[...], preferred_element_type=f32)
            shaped = jnp.stack([mixed[:, t * 128:(t + 1) * 128].reshape(32, 8, 128) for t in range(8)], axis=1)
            shaped = shaped.reshape(2048, 128).astype(bf16)
            for g in range(4):
                pair = jnp.concatenate(
                    [shaped[g * 512:g * 512 + 256], shaped[g * 512 + 256:g * 512 + 512]], axis=1)
                out = jnp.dot(coupler[...], pair, preferred_element_type=f32)
                for h in range(2):
                    half = out[:, h * 128:(h + 1) * 128].reshape(4, 8, 8, 128)
                    for u in range(8):
                        target[pl.ds(i * 256 + g * 64 + h * 32, 32), u * 128:(u + 1) * 128] = (
                            half[:, u].reshape(32, 128).astype(bf16))
            return carry
        lax.fori_loop(0, 4, step, 0)

    def remote(source, target, phase, slot, peer):
        copy = pltpu.make_async_remote_copy(
            src_ref=source, dst_ref=target, send_sem=block_send.at[phase, slot], recv_sem=block_recv.at[phase, slot],
            device_id=(seg, peer), device_id_type=MESH)
        copy.start()
        pending.append(copy)
        return copy

    def rows_of(k, column):
        return pl.ds(pl.multiple_of((row_order[k] * SIDE + column) * rows, rows), rows)

    def image(source, vector, sent, side, phase, scale, first, more):
        lanes = slice(first, 1024)
        dots = jnp.zeros((8, 128), f32)
        copies = []
        for k in range(ROW):
            span = pl.ds(pl.multiple_of(row_order[k] * 256, 256), 256)
            part = jnp.dot(source[span, lanes], stacked[lanes, :], preferred_element_type=f32)
            if more:
                part = part + partial[span, :]
            dots = dots + jnp.sum((part * vector[span, :].astype(f32)).reshape(32, 8, 128), axis=0)
            if scale is not None:
                part = part * scale
            partial[span, :] = part
            sent[span, :] = part.astype(bf16)
            for j in (2, 1, 3):
                column = lax.rem(place + j, SIDE)
                slot = k * 3 + j - 1
                copies.append(remote(
                    sent.at[rows_of(k, column), :], side.at[slot], phase, slot, row * SIDE + column))
        return total(dots), copies

    def along_z(phase, copies, side, sent, target):
        onward = []
        for k in range(ROW):
            value = partial[rows_of(k, place), :]
            for copy in copies[3 * k:3 * k + 3]:
                copy.wait_recv()
            for slot in range(3 * k, 3 * k + 3):
                value = value + side[slot].astype(f32)
            if k < 3:
                sent[k] = value.astype(bf16)
                onward.append(remote(sent.at[k], target.at[k], phase, 12 + k, row_order[k] * SIDE + place))
        return value, onward

    def scatter_sum(value, onward, target):
        for k in (2, 1, 0):
            onward[k].wait_recv()
            value = value + target[k].astype(f32)
        return value

    def grow(pairs, target):
        for u in range(0, 8, 2):
            lanes = slice(u * 128, (u + 2) * 128)
            value = None
            for transposed, source in pairs:
                term = jnp.dot(transposed[...], source[:, lanes], preferred_element_type=f32)
                value = term if value is None else value + term
            target[pl.ds(u, 128, stride=8), :] = value[:, :128]
            target[pl.ds(u + 1, 128, stride=8), :] = value[:, 128:]

    def scalar_round(phase, value):
        scal_send[phase] = jnp.broadcast_to(value, (1, 128))
        copies = []
        for step, peer in enumerate(peers):
            copies.append(pltpu.make_async_remote_copy(
                src_ref=scal_send.at[phase], dst_ref=scal_recv.at[phase, me],
                send_sem=scal_send_sem.at[phase, step], recv_sem=scal_recv_sem.at[phase, step],
                device_id=(seg, peer), device_id_type=MESH))
            copies[-1].start()
        scal_recv[phase, me] = scal_send[phase]
        return copies

    def scalar_sum(phase, copies):
        for copy in copies:
            copy.wait()
        return jnp.sum(scal_recv[phase], axis=0)[:, :1]

    own = pl.ds(pl.multiple_of(me * rows, rows), rows)

    loads[1].wait()
    spread[...] = start[...].astype(f32)
    for t in range(8):
        wide[:, t * 128:(t + 1) * 128] = spread[pl.ds(t, 128, stride=8), :].astype(bf16)
    norm = total(jnp.sum((spread[...] * spread[...]).reshape(-1, 8, 128), axis=0))
    inverse = 1.0 / jnp.sqrt(norm / entries + epsilon)
    loads[3].wait()
    spot = lax.broadcasted_iota(jnp.int32, (8, 256), 0)
    wide_lane = lax.broadcasted_iota(jnp.int32, (8, 256), 1)
    compact = jnp.zeros((64, 256), f32)
    for w in range(8):
        chosen = jnp.where(lax.rem(wide_lane, 64) == spot * 8 + w, 1.0, 0.0).astype(f32)
        compact = compact + jnp.dot(
            mpo[w].astype(f32).reshape(64, 8), chosen, preferred_element_type=f32)
    tall = jnp.concatenate([compact] * 4, axis=0)
    row_group = lax.broadcasted_iota(jnp.int32, (256, 256), 0) // 64
    lane_group = lax.broadcasted_iota(jnp.int32, (256, 256), 1) // 64
    coupler[...] = jnp.where(row_group == lane_group, tall, 0.0).astype(bf16)
    loads[2].wait()
    couple(coupled_1)
    start_t[...] = jnp.transpose(start[...])

    ring[0].wait_recv()
    for c in range(CHUNKS):
        ring[1 + c].wait_recv()
        for u in range(c * share, (c + 1) * share):
            unpack(u)
        if c < CHUNKS - 1:
            def add(i, carry, c=c):
                span, lanes = pl.ds(i * 256, 256), slice(c * share * 128, (c + 1) * share * 128)
                part = jnp.dot(coupled_1[span, lanes], stacked[lanes, :], preferred_element_type=f32)
                partial[span, :] = part if c == 0 else partial[span, :] + part
                return carry
            lax.fori_loop(0, 4, add, 0)
    ray, copies = image(coupled_1, start, send_1, side_1, 0, None, (CHUNKS - 1) * share * 128, True)
    pl.when(row < ROW - 1)(lambda: pl.semaphore_wait(ready, SIDE * (ROW - 1 - row)))
    ray_copies = scalar_round(0, ray)
    grow([(start_t, coupled_1)], grown_11)
    @pl.when(early)
    def _():
        pl.semaphore_wait(distant, 1)
        for copy in ring:
            copy.start()

    value, onward = along_z(0, copies, side_1, sums_1, recv_1)
    rayleigh = scalar_sum(0, ray_copies) * (inverse * inverse / entries)
    image_1 = scatter_sum(value, onward, recv_1)
    block = inverse * image_1 - (rayleigh * inverse) * start[own, :].astype(f32)
    resid[own, :] = block.astype(bf16)

    def spread_out(k):
        held = resid.at[rows_of(k, place), :]
        return [remote(held, held, 1, k * 3 + j - 1, row * SIDE + lax.rem(place + j, SIDE)) for j in (2, 1, 3)]

    mine = resid.at[own, :]
    onward = [remote(mine, mine, 1, 12 + k, row_order[k] * SIDE + place) for k in range(3)]
    relayed = {3: spread_out(3)}
    size_copies = scalar_round(1, total(block * block))
    for k in (2, 1, 0):
        onward[k].wait_recv()
        relayed[k] = spread_out(k)

    for k in (3, 2, 1, 0):
        for copy in relayed[k]:
            copy.wait_recv()
        span = pl.ds(pl.multiple_of(row_order[k] * 256, 256), 256)
        spread[span, :] = resid[span, :].astype(f32)
        for t in range(8):
            wide[pl.ds(pl.multiple_of(row_order[k] * 32, 32), 32), t * 128:(t + 1) * 128] = (
                spread[pl.ds(row_order[k] * 256 + t, 32, stride=8), :].astype(bf16))

    couple(coupled_2)
    size = jnp.sqrt(scalar_sum(1, size_copies) / entries + epsilon)
    curve, copies = image(coupled_2, resid, send_2, side_2, 2, 1.0 / size, 0, False)
    curve_copies = scalar_round(2, curve)
    resid_t[...] = jnp.transpose(resid[...])
    grow([(start_t, coupled_2), (resid_t, coupled_1)], grown_x)
    value, onward = along_z(2, copies, side_2, sums_2, recv_2)
    grow([(resid_t, coupled_2)], grown_22)
    curvature = scalar_sum(2, curve_copies) / (size * size * entries)
    middle = 0.5 * (rayleigh + curvature)
    half_gap = 0.5 * (rayleigh - curvature)
    lowest = middle - jnp.sqrt(half_gap * half_gap + size * size)
    offset = lowest - rayleigh
    length = jnp.sqrt(size * size + offset * offset)
    first = size / length * inverse
    second = offset / length / size
    energy_ref[...] = jnp.broadcast_to(lowest, (8, 128))
    state_ref[...] = (first * start[...].astype(f32) + second * resid[...].astype(f32)).astype(bf16)
    grown_ref[...] = (first * first * grown_11[...] + first * second * grown_x[...]
                      + second * second * grown_22[...]).astype(bf16)
    for copy in ring + pending:
        copy.wait_send()
    image_ref[...] = scatter_sum(value, onward, recv_2)


def write_out(state, grown, energy, image, state_out, grown_out, energy_out, image_out, sems):
    copies = [
        pltpu.make_async_copy(source, target, sems.at[spot])
        for spot, (source, target) in enumerate(((state, state_out), (grown, grown_out), (image, image_out)))
    ]
    for copy in copies:
        copy.start()
    energy_out[0] = energy[0, 0]
    for copy in copies:
        copy.wait()


def solution(mesh):
    segs, bonds = mesh.shape["seg"], mesh.shape["bond"]

    def body(left_env, right_env, mpo_site, start_state):
        big, half = (1024, 128), (1024 // bonds, 128)
        anywhere = pl.BlockSpec(memory_space=pl.ANY)
        vmem = pl.BlockSpec(memory_space=pltpu.VMEM)
        results = pl.pallas_call(
            lambda *refs: kernel(segs, bonds, *refs),
            out_shape=(pltpu.VMEM(big, bf16), pltpu.VMEM(big, bf16), pltpu.VMEM((8, 128), f32), pltpu.VMEM(half, f32)),
            in_specs=[pl.BlockSpec(memory_space=pltpu.HBM)] * 4,
            out_specs=(vmem,) * 4,
            scratch_shapes=[
                pltpu.VMEM(big, bf16),
                pltpu.VMEM(big, bf16),
                pltpu.VMEM((8, 8, 8, 8), bf16),
                pltpu.VMEM(big, bf16),
                pltpu.VMEM(big, f32),
                pltpu.VMEM((128, 1024), bf16),
                pltpu.VMEM(big, bf16),
                pltpu.VMEM((256, 256), bf16),
                pltpu.VMEM((8, 64, 128), bf16),
                pltpu.VMEM((8, 64, 128), bf16),
                pltpu.VMEM((8, 128), f32),
                pltpu.VMEM((8, 128), f32),
                pltpu.VMEM((1024, 1024), bf16),
                pltpu.VMEM((1024, 1024), bf16),
                pltpu.VMEM(big, f32),
                pltpu.VMEM((128, 1024), bf16),
                pltpu.VMEM((128, 1024), bf16),
                pltpu.VMEM(big, bf16),
                pltpu.VMEM(big, bf16),
                pltpu.VMEM((12,) + half, bf16),
                pltpu.VMEM((12,) + half, bf16),
                pltpu.VMEM((3,) + half, bf16),
                pltpu.VMEM((3,) + half, bf16),
                pltpu.VMEM((3,) + half, bf16),
                pltpu.VMEM((3,) + half, bf16),
                pltpu.VMEM(big, bf16),
                pltpu.VMEM((3, 1, 128), f32),
                pltpu.VMEM((3, bonds, 1, 128), f32),
                pltpu.VMEM(big, f32),
                pltpu.VMEM(big, f32),
                pltpu.VMEM(big, f32),
                pltpu.SemaphoreType.REGULAR,
                pltpu.SemaphoreType.REGULAR,
                pltpu.SemaphoreType.DMA((4,)),
                pltpu.SemaphoreType.DMA((CHUNKS + 1,)),
                pltpu.SemaphoreType.DMA((CHUNKS + 1,)),
                pltpu.SemaphoreType.DMA((3, bonds - 1)),
                pltpu.SemaphoreType.DMA((3, bonds - 1)),
                pltpu.SemaphoreType.DMA((3, bonds - 1)),
                pltpu.SemaphoreType.DMA((3, bonds - 1)),
            ],
            compiler_params=pltpu.CompilerParams(
                collective_id=0, has_side_effects=True, vmem_limit_bytes=32 * 1024 * 1024),
            name="ritz_step",
        )(*(pltpu.with_memory_space_constraint(x, pltpu.HBM) for x in (
            left_env.reshape(big), right_env.reshape(big), mpo_site[0], start_state.reshape(big))))
        state, grown, energy, image = pl.pallas_call(
            write_out,
            out_shape=(
                jax.ShapeDtypeStruct(big, bf16),
                jax.ShapeDtypeStruct(big, bf16),
                jax.ShapeDtypeStruct((1,), f32),
                jax.ShapeDtypeStruct(half, f32),
            ),
            in_specs=[vmem] * 4,
            out_specs=(anywhere, anywhere, pl.BlockSpec(memory_space=pltpu.SMEM), anywhere),
            scratch_shapes=[pltpu.SemaphoreType.DMA((3,))],
            compiler_params=pltpu.CompilerParams(vmem_limit_bytes=8 * 1024 * 1024),
            name="write_out",
        )(*results)
        return (
            state.reshape(1, 128, 8, 128),
            grown.reshape(1, 128, 8, 128),
            energy,
            image.reshape(1, 1024 // bonds // 8, 8, 128),
        )

    in_specs = (
        P("seg", None, "bond", None),
        P("seg", None, "bond", None),
        P("seg", "bond", None, None, None),
        P("seg", None, None, None),
    )
    out_specs = (
        P("seg", None, None, None),
        P("seg", None, "bond", None),
        P("seg"),
        P("seg", "bond", None, None),
    )
    return jax.shard_map(body, mesh=mesh, in_specs=in_specs, out_specs=out_specs, check_vma=False)
```

```python
import jax
import jax.numpy as jnp
from jax import lax
from jax.experimental import pallas as pl
from jax.experimental.pallas import tpu as pltpu
from jax.sharding import PartitionSpec as P

epsilon = 1e-06
MESH = pl.DeviceIdType.MESH
f32, bf16 = jnp.float32, jnp.bfloat16
ROW, SIDE = 4, 4
CHUNKS = 2


def total(value):
    return jnp.sum(jnp.sum(value, axis=1, keepdims=True), axis=0, keepdims=True)


def kernel(segs, bonds, left_hbm, right_hbm, mpo_hbm, start_hbm,
           state_ref, grown_ref, energy_ref, image_ref,
           left, right, mpo, start, spread, wide, stacked, coupler, pack_send, pack_recv, edge_send, edge_recv,
           coupled_1, coupled_2, partial, start_t, resid_t,
           send_1, send_2, side_1, side_2, sums_1, sums_2, recv_1, recv_2, resid, scal_send, scal_recv,
           grown_11, grown_x, grown_22,
           ready, distant, local_sem, ring_send, ring_recv, block_send, block_recv, scal_send_sem, scal_recv_sem):
    seg, me = lax.axis_index("seg"), lax.axis_index("bond")
    before, after = lax.rem(seg + segs - 1, segs), lax.rem(seg + 1, segs)
    rows = partial.shape[0] // bonds
    entries = partial.shape[0] * partial.shape[1]
    row, place = me // SIDE, lax.rem(me, SIDE)
    row_order = [3 - row, lax.rem(row + 2, ROW), row + 1 - 2 * lax.rem(row, 2), row]
    peers = []
    for k, other in enumerate(row_order):
        for j in (2, 1, 3, 0):
            if k < 3 or j:
                peers.append(other * SIDE + lax.rem(place + j, SIDE))
    pending = []

    loads = [
        pltpu.make_async_copy(source, target, local_sem.at[spot])
        for spot, (source, target) in enumerate(
            ((right_hbm, right), (start_hbm, start), (left_hbm, left), (mpo_hbm, mpo)))
    ]
    for load in loads:
        load.start()

    early, late = lax.rem(seg, 8) == 0, lax.rem(seg, 8) == 7
    barrier = pltpu.get_barrier_semaphore()

    def enter(device, semaphore=barrier):
        pl.semaphore_signal(semaphore, inc=1, device_id=device, device_id_type=MESH)

    pl.when(jnp.logical_not(late))(lambda: enter((after, me)))
    pl.when(early)(lambda: enter((before, me)))
    for peer in peers:
        pl.when(peer > me)(lambda peer=peer: enter((seg, peer)))

    up = lax.broadcasted_iota(jnp.int32, (64, 128), 0)
    lane = lax.broadcasted_iota(jnp.int32, (64, 128), 1)
    keep = jnp.where(lane < 64, jnp.where(lane <= up, 1, 0), jnp.where(lane - 64 > up, 1, 0)) == 1
    near, far = lane == up, lane == up + 64
    loads[0].wait()
    spread[...] = right[...].astype(f32)
    for u in range(8):
        low = spread[pl.ds(u, 64, stride=8), :]
        high = spread[pl.ds(512 + u, 64, stride=8), :]
        pack_send[u] = jnp.where(keep, low, high).astype(bf16)
        edge_send[u:u + 1, :] = jnp.sum(
            jnp.where(far, low, 0.0) + jnp.where(near, high, 0.0), axis=0, keepdims=True)
    ahead = me + 1 - jnp.where(early, 1, 0) + jnp.where(late, 1, 0)
    pl.when(ahead > 0)(lambda: pl.semaphore_wait(barrier, ahead))
    pl.when(late)(lambda: enter((after, me), distant))

    share = 8 // CHUNKS
    ring = [pltpu.make_async_remote_copy(
        src_ref=edge_send, dst_ref=edge_recv, send_sem=ring_send.at[CHUNKS], recv_sem=ring_recv.at[CHUNKS],
        device_id=(before, me), device_id_type=MESH)]
    for c in range(CHUNKS):
        part = pl.ds(c * share, share)
        ring.append(pltpu.make_async_remote_copy(
            src_ref=pack_send.at[part], dst_ref=pack_recv.at[part],
            send_sem=ring_send.at[c], recv_sem=ring_recv.at[c],
            device_id=(before, me), device_id_type=MESH))

    @pl.when(jnp.logical_not(early))
    def _():
        for copy in ring:
            copy.start()

    for peer in peers:
        pl.when(peer < me)(lambda peer=peer: enter((seg, peer), ready))

    def unpack(u):
        half = pack_recv[u].astype(f32)
        turned = jnp.transpose(jnp.concatenate([half, half], axis=0))
        edge = jnp.broadcast_to(edge_recv[u:u + 1, :], (64, 128))
        top = jnp.where(far, edge, jnp.where(keep, half, turned[:64]))
        low = jnp.where(near, edge, jnp.where(keep, turned[64:], half))
        stacked[u * 128:u * 128 + 64, :] = top.astype(bf16)
        stacked[u * 128 + 64:u * 128 + 128, :] = low.astype(bf16)

    def couple(target):
        def step(i):
            mixed = jnp.dot(left[pl.ds(i * 256, 256), :], wide[...], preferred_element_type=f32)
            shaped = jnp.stack([mixed[:, t * 128:(t + 1) * 128].reshape(32, 8, 128) for t in range(8)], axis=1)
            shaped = shaped.reshape(2048, 128).astype(bf16)
            for g in range(4):
                pair = jnp.concatenate(
                    [shaped[g * 512:g * 512 + 256], shaped[g * 512 + 256:g * 512 + 512]], axis=1)
                out = jnp.dot(coupler[...], pair, preferred_element_type=f32)
                for h in range(2):
                    half = out[:, h * 128:(h + 1) * 128].reshape(4, 8, 8, 128)
                    for u in range(8):
                        target[pl.ds(i * 256 + g * 64 + h * 32, 32), u * 128:(u + 1) * 128] = (
                            half[:, u].reshape(32, 128).astype(bf16))
        for i in range(4):
            step(i)

    def remote(source, target, phase, slot, peer):
        copy = pltpu.make_async_remote_copy(
            src_ref=source, dst_ref=target, send_sem=block_send.at[phase, slot], recv_sem=block_recv.at[phase, slot],
            device_id=(seg, peer), device_id_type=MESH)
        copy.start()
        pending.append(copy)
        return copy

    def rows_of(k, column):
        return pl.ds(pl.multiple_of((row_order[k] * SIDE + column) * rows, rows), rows)

    def image(source, vector, sent, side, phase, scale, first, more):
        lanes = slice(first, 1024)
        dots = jnp.zeros((8, 128), f32)
        copies = []
        for k in range(ROW):
            span = pl.ds(pl.multiple_of(row_order[k] * 256, 256), 256)
            part = jnp.dot(source[span, lanes], stacked[lanes, :], preferred_element_type=f32)
            if more:
                part = part + partial[span, :]
            dots = dots + jnp.sum((part * vector[span, :].astype(f32)).reshape(32, 8, 128), axis=0)
            if scale is not None:
                part = part * scale
            partial[span, :] = part
            sent[span, :] = part.astype(bf16)
            for j in (2, 1, 3):
                column = lax.rem(place + j, SIDE)
                slot = k * 3 + j - 1
                copies.append(remote(
                    sent.at[rows_of(k, column), :], side.at[slot], phase, slot, row * SIDE + column))
        return total(dots), copies

    def along_z(phase, copies, side, sent, target):
        onward = []
        for k in range(ROW):
            value = partial[rows_of(k, place), :]
            for copy in copies[3 * k:3 * k + 3]:
                copy.wait_recv()
            for slot in range(3 * k, 3 * k + 3):
                value = value + side[slot].astype(f32)
            if k < 3:
                sent[k] = value.astype(bf16)
                onward.append(remote(sent.at[k], target.at[k], phase, 12 + k, row_order[k] * SIDE + place))
        return value, onward

    def scatter_sum(value, onward, target):
        for k in (2, 1, 0):
            onward[k].wait_recv()
            value = value + target[k].astype(f32)
        return value

    def grow(pairs, target):
        for u in range(0, 8, 2):
            lanes = slice(u * 128, (u + 2) * 128)
            value = None
            for transposed, source in pairs:
                term = jnp.dot(transposed[...], source[:, lanes], preferred_element_type=f32)
                value = term if value is None else value + term
            target[pl.ds(u, 128, stride=8), :] = value[:, :128]
            target[pl.ds(u + 1, 128, stride=8), :] = value[:, 128:]

    def scalar_round(phase, value):
        scal_send[phase] = jnp.broadcast_to(value, (1, 128))
        copies = []
        for step, peer in enumerate(peers):
            copies.append(pltpu.make_async_remote_copy(
                src_ref=scal_send.at[phase], dst_ref=scal_recv.at[phase, me],
                send_sem=scal_send_sem.at[phase, step], recv_sem=scal_recv_sem.at[phase, step],
                device_id=(seg, peer), device_id_type=MESH))
            copies[-1].start()
        scal_recv[phase, me] = scal_send[phase]
        return copies

    def scalar_sum(phase, copies):
        for copy in copies:
            copy.wait()
        return jnp.sum(scal_recv[phase], axis=0)[:, :1]

    own = pl.ds(pl.multiple_of(me * rows, rows), rows)

    loads[1].wait()
    spread[...] = start[...].astype(f32)
    for t in range(8):
        wide[:, t * 128:(t + 1) * 128] = spread[pl.ds(t, 128, stride=8), :].astype(bf16)
    norm = total(jnp.sum((spread[...] * spread[...]).reshape(-1, 8, 128), axis=0))
    inverse = 1.0 / jnp.sqrt(norm / entries + epsilon)
    loads[3].wait()
    spot = lax.broadcasted_iota(jnp.int32, (8, 256), 0)
    wide_lane = lax.broadcasted_iota(jnp.int32, (8, 256), 1)
    compact = jnp.zeros((64, 256), f32)
    for w in range(8):
        chosen = jnp.where(lax.rem(wide_lane, 64) == spot * 8 + w, 1.0, 0.0).astype(f32)
        compact = compact + jnp.dot(
            mpo[w].astype(f32).reshape(64, 8), chosen, preferred_element_type=f32)
    tall = jnp.concatenate([compact] * 4, axis=0)
    row_group = lax.broadcasted_iota(jnp.int32, (256, 256), 0) // 64
    lane_group = lax.broadcasted_iota(jnp.int32, (256, 256), 1) // 64
    coupler[...] = jnp.where(row_group == lane_group, tall, 0.0).astype(bf16)
    loads[2].wait()
    couple(coupled_1)
    start_t[...] = jnp.transpose(start[...])

    ring[0].wait_recv()
    for c in range(CHUNKS):
        ring[1 + c].wait_recv()
        for u in range(c * share, (c + 1) * share):
            unpack(u)
        if c < CHUNKS - 1:
            def add(i, carry, c=c):
                span, lanes = pl.ds(i * 256, 256), slice(c * share * 128, (c + 1) * share * 128)
                part = jnp.dot(coupled_1[span, lanes], stacked[lanes, :], preferred_element_type=f32)
                partial[span, :] = part if c == 0 else partial[span, :] + part
                return carry
            lax.fori_loop(0, 4, add, 0)
    pl.when(me < bonds - 1)(lambda: pl.semaphore_wait(ready, bonds - 1 - me))
    ray, copies = image(coupled_1, start, send_1, side_1, 0, None, (CHUNKS - 1) * share * 128, True)
    ray_copies = scalar_round(0, ray)
    grow([(start_t, coupled_1)], grown_11)
    @pl.when(early)
    def _():
        pl.semaphore_wait(distant, 1)
        for copy in ring:
            copy.start()

    value, onward = along_z(0, copies, side_1, sums_1, recv_1)
    rayleigh = scalar_sum(0, ray_copies) * (inverse * inverse / entries)
    image_1 = scatter_sum(value, onward, recv_1)
    block = inverse * image_1 - (rayleigh * inverse) * start[own, :].astype(f32)
    resid[own, :] = block.astype(bf16)

    def spread_out(k):
        held = resid.at[rows_of(k, place), :]
        return [remote(held, held, 1, k * 3 + j - 1, row * SIDE + lax.rem(place + j, SIDE)) for j in (2, 1, 3)]

    mine = resid.at[own, :]
    onward = [remote(mine, mine, 1, 12 + k, row_order[k] * SIDE + place) for k in range(3)]
    relayed = {3: spread_out(3)}
    size_copies = scalar_round(1, total(block * block))
    for k in (2, 1, 0):
        onward[k].wait_recv()
        relayed[k] = spread_out(k)

    for k in (3, 2, 1, 0):
        for copy in relayed[k]:
            copy.wait_recv()
        span = pl.ds(pl.multiple_of(row_order[k] * 256, 256), 256)
        spread[span, :] = resid[span, :].astype(f32)
        for t in range(8):
            wide[pl.ds(pl.multiple_of(row_order[k] * 32, 32), 32), t * 128:(t + 1) * 128] = (
                spread[pl.ds(row_order[k] * 256 + t, 32, stride=8), :].astype(bf16))

    couple(coupled_2)
    size = jnp.sqrt(scalar_sum(1, size_copies) / entries + epsilon)
    curve, copies = image(coupled_2, resid, send_2, side_2, 2, 1.0 / size, 0, False)
    curve_copies = scalar_round(2, curve)
    resid_t[...] = jnp.transpose(resid[...])
    grow([(start_t, coupled_2), (resid_t, coupled_1)], grown_x)
    value, onward = along_z(2, copies, side_2, sums_2, recv_2)
    grow([(resid_t, coupled_2)], grown_22)
    curvature = scalar_sum(2, curve_copies) / (size * size * entries)
    middle = 0.5 * (rayleigh + curvature)
    half_gap = 0.5 * (rayleigh - curvature)
    lowest = middle - jnp.sqrt(half_gap * half_gap + size * size)
    offset = lowest - rayleigh
    length = jnp.sqrt(size * size + offset * offset)
    first = size / length * inverse
    second = offset / length / size
    energy_ref[...] = jnp.broadcast_to(lowest, (8, 128))
    state_ref[...] = (first * start[...].astype(f32) + second * resid[...].astype(f32)).astype(bf16)
    grown_ref[...] = (first * first * grown_11[...] + first * second * grown_x[...]
                      + second * second * grown_22[...]).astype(bf16)
    for copy in ring + pending:
        copy.wait_send()
    image_ref[...] = scatter_sum(value, onward, recv_2)


def write_out(state, grown, energy, image, state_out, grown_out, energy_out, image_out, lowest, sems):
    copies = [
        pltpu.make_async_copy(source, target, sems.at[spot])
        for spot, (source, target) in enumerate(((state, state_out), (grown, grown_out), (image, image_out)))
    ]
    for copy in copies:
        copy.start()
    lowest[0] = energy[0, 0]
    copies.append(pltpu.make_async_copy(lowest, energy_out, sems.at[3]))
    copies[3].start()
    for copy in copies:
        copy.wait()


def solution(mesh):
    segs, bonds = mesh.shape["seg"], mesh.shape["bond"]

    def body(left_env, right_env, mpo_site, start_state):
        big, half = (1024, 128), (1024 // bonds, 128)
        anywhere = pl.BlockSpec(memory_space=pl.ANY)
        vmem = pl.BlockSpec(memory_space=pltpu.VMEM)
        results = pl.pallas_call(
            lambda *refs: kernel(segs, bonds, *refs),
            out_shape=(pltpu.VMEM(big, bf16), pltpu.VMEM(big, bf16), pltpu.VMEM((8, 128), f32), pltpu.VMEM(half, f32)),
            in_specs=[pl.BlockSpec(memory_space=pltpu.HBM)] * 4,
            out_specs=(vmem,) * 4,
            scratch_shapes=[
                pltpu.VMEM(big, bf16),
                pltpu.VMEM(big, bf16),
                pltpu.VMEM((8, 8, 8, 8), bf16),
                pltpu.VMEM(big, bf16),
                pltpu.VMEM(big, f32),
                pltpu.VMEM((128, 1024), bf16),
                pltpu.VMEM(big, bf16),
                pltpu.VMEM((256, 256), bf16),
                pltpu.VMEM((8, 64, 128), bf16),
                pltpu.VMEM((8, 64, 128), bf16),
                pltpu.VMEM((8, 128), f32),
                pltpu.VMEM((8, 128), f32),
                pltpu.VMEM((1024, 1024), bf16),
                pltpu.VMEM((1024, 1024), bf16),
                pltpu.VMEM(big, f32),
                pltpu.VMEM((128, 1024), bf16),
                pltpu.VMEM((128, 1024), bf16),
                pltpu.VMEM(big, bf16),
                pltpu.VMEM(big, bf16),
                pltpu.VMEM((12,) + half, bf16),
                pltpu.VMEM((12,) + half, bf16),
                pltpu.VMEM((3,) + half, bf16),
                pltpu.VMEM((3,) + half, bf16),
                pltpu.VMEM((3,) + half, bf16),
                pltpu.VMEM((3,) + half, bf16),
                pltpu.VMEM(big, bf16),
                pltpu.VMEM((3, 1, 128), f32),
                pltpu.VMEM((3, bonds, 1, 128), f32),
                pltpu.VMEM(big, f32),
                pltpu.VMEM(big, f32),
                pltpu.VMEM(big, f32),
                pltpu.SemaphoreType.REGULAR,
                pltpu.SemaphoreType.REGULAR,
                pltpu.SemaphoreType.DMA((4,)),
                pltpu.SemaphoreType.DMA((CHUNKS + 1,)),
                pltpu.SemaphoreType.DMA((CHUNKS + 1,)),
                pltpu.SemaphoreType.DMA((3, bonds - 1)),
                pltpu.SemaphoreType.DMA((3, bonds - 1)),
                pltpu.SemaphoreType.DMA((3, bonds - 1)),
                pltpu.SemaphoreType.DMA((3, bonds - 1)),
            ],
            compiler_params=pltpu.CompilerParams(
                collective_id=0, has_side_effects=True, vmem_limit_bytes=32 * 1024 * 1024),
            name="ritz_step",
        )(*(pltpu.with_memory_space_constraint(x, pltpu.HBM) for x in (
            left_env.reshape(big), right_env.reshape(big), mpo_site[0], start_state.reshape(big))))
        state, grown, energy, image = pl.pallas_call(
            write_out,
            out_shape=(
                jax.ShapeDtypeStruct(big, bf16),
                jax.ShapeDtypeStruct(big, bf16),
                jax.ShapeDtypeStruct((1,), f32),
                jax.ShapeDtypeStruct(half, f32),
            ),
            in_specs=[vmem] * 4,
            out_specs=(anywhere,) * 4,
            scratch_shapes=[pltpu.SMEM((1,), f32), pltpu.SemaphoreType.DMA((4,))],
            compiler_params=pltpu.CompilerParams(vmem_limit_bytes=8 * 1024 * 1024),
            name="write_out",
        )(*results)
        return (
            state.reshape(1, 128, 8, 128),
            grown.reshape(1, 128, 8, 128),
            energy,
            image.reshape(1, 1024 // bonds // 8, 8, 128),
        )

    in_specs = (
        P("seg", None, "bond", None),
        P("seg", None, "bond", None),
        P("seg", "bond", None, None, None),
        P("seg", None, None, None),
    )
    out_specs = (
        P("seg", None, None, None),
        P("seg", None, "bond", None),
        P("seg"),
        P("seg", "bond", None, None),
    )
    return jax.shard_map(body, mesh=mesh, in_specs=in_specs, out_specs=out_specs, check_vma=False)
```

```python
import jax
import jax.numpy as jnp
from jax import lax
from jax.experimental import pallas as pl
from jax.experimental.pallas import tpu as pltpu
from jax.sharding import PartitionSpec as P

epsilon = 1e-06
MESH = pl.DeviceIdType.MESH
f32, bf16 = jnp.float32, jnp.bfloat16
ROW, SIDE = 4, 4
CHUNKS = 2


def total(value):
    return jnp.sum(jnp.sum(value, axis=1, keepdims=True), axis=0, keepdims=True)


def kernel(segs, bonds, left_hbm, right_hbm, mpo_hbm, start_hbm,
           state_ref, grown_ref, energy_ref, image_ref,
           left, right, mpo, start, spread, wide, stacked, coupler, pack_send, pack_recv, edge_send, edge_recv,
           coupled_1, coupled_2, partial, start_t, resid_t,
           send_1, send_2, side_1, side_2, sums_1, sums_2, recv_1, recv_2, resid, scal_send, scal_recv,
           grown_11, grown_x, grown_22,
           ready, distant, local_sem, ring_send, ring_recv, block_send, block_recv, scal_send_sem, scal_recv_sem):
    seg, me = lax.axis_index("seg"), lax.axis_index("bond")
    before, after = lax.rem(seg + segs - 1, segs), lax.rem(seg + 1, segs)
    rows = partial.shape[0] // bonds
    entries = partial.shape[0] * partial.shape[1]
    row, place = me // SIDE, lax.rem(me, SIDE)
    row_order = [3 - row, lax.rem(row + 2, ROW), row + 1 - 2 * lax.rem(row, 2), row]
    peers = []
    for k, other in enumerate(row_order):
        for j in (2, 1, 3, 0):
            if k < 3 or j:
                peers.append(other * SIDE + lax.rem(place + j, SIDE))
    pending = []

    loads = [
        pltpu.make_async_copy(source, target, local_sem.at[spot])
        for spot, (source, target) in enumerate(
            ((right_hbm, right), (start_hbm, start), (left_hbm, left), (mpo_hbm, mpo)))
    ]
    for load in loads:
        load.start()

    early, late = lax.rem(seg, 8) == 0, lax.rem(seg, 8) == 7
    barrier = pltpu.get_barrier_semaphore()

    def enter(device, semaphore=barrier):
        pl.semaphore_signal(semaphore, inc=1, device_id=device, device_id_type=MESH)

    pl.when(jnp.logical_not(late))(lambda: enter((after, me)))
    pl.when(early)(lambda: enter((before, me)))
    for peer in peers:
        pl.when(peer > me)(lambda peer=peer: enter((seg, peer)))

    up = lax.broadcasted_iota(jnp.int32, (64, 128), 0)
    lane = lax.broadcasted_iota(jnp.int32, (64, 128), 1)
    keep = jnp.where(lane < 64, jnp.where(lane <= up, 1, 0), jnp.where(lane - 64 > up, 1, 0)) == 1
    near, far = lane == up, lane == up + 64
    loads[0].wait()
    spread[...] = right[...].astype(f32)
    for u in range(8):
        low = spread[pl.ds(u, 64, stride=8), :]
        high = spread[pl.ds(512 + u, 64, stride=8), :]
        pack_send[u] = jnp.where(keep, low, high).astype(bf16)
        edge_send[u:u + 1, :] = jnp.sum(
            jnp.where(far, low, 0.0) + jnp.where(near, high, 0.0), axis=0, keepdims=True)
    ahead = me + 1 - jnp.where(early, 1, 0) + jnp.where(late, 1, 0)
    pl.when(ahead > 0)(lambda: pl.semaphore_wait(barrier, ahead))
    pl.when(late)(lambda: enter((after, me), distant))

    share = 8 // CHUNKS
    ring = [pltpu.make_async_remote_copy(
        src_ref=edge_send, dst_ref=edge_recv, send_sem=ring_send.at[CHUNKS], recv_sem=ring_recv.at[CHUNKS],
        device_id=(before, me), device_id_type=MESH)]
    for c in range(CHUNKS):
        part = pl.ds(c * share, share)
        ring.append(pltpu.make_async_remote_copy(
            src_ref=pack_send.at[part], dst_ref=pack_recv.at[part],
            send_sem=ring_send.at[c], recv_sem=ring_recv.at[c],
            device_id=(before, me), device_id_type=MESH))

    @pl.when(jnp.logical_not(early))
    def _():
        for copy in ring:
            copy.start()

    for peer in peers:
        pl.when(peer < me)(lambda peer=peer: enter((seg, peer), ready))

    def unpack(u):
        half = pack_recv[u].astype(f32)
        turned = jnp.transpose(jnp.concatenate([half, half], axis=0))
        edge = jnp.broadcast_to(edge_recv[u:u + 1, :], (64, 128))
        top = jnp.where(far, edge, jnp.where(keep, half, turned[:64]))
        low = jnp.where(near, edge, jnp.where(keep, turned[64:], half))
        stacked[u * 128:u * 128 + 64, :] = top.astype(bf16)
        stacked[u * 128 + 64:u * 128 + 128, :] = low.astype(bf16)

    def couple(i, target):
        mixed = jnp.dot(left[pl.ds(i * 256, 256), :], wide[...], preferred_element_type=f32)
        shaped = jnp.stack([mixed[:, t * 128:(t + 1) * 128].reshape(32, 8, 128) for t in range(8)], axis=1)
        shaped = shaped.reshape(2048, 128).astype(bf16)
        for g in range(4):
            pair = jnp.concatenate(
                [shaped[g * 512:g * 512 + 256], shaped[g * 512 + 256:g * 512 + 512]], axis=1)
            out = jnp.dot(coupler[...], pair, preferred_element_type=f32)
            for h in range(2):
                half = out[:, h * 128:(h + 1) * 128].reshape(4, 8, 8, 128)
                for u in range(8):
                    target[pl.ds(i * 256 + g * 64 + h * 32, 32), u * 128:(u + 1) * 128] = (
                        half[:, u].reshape(32, 128).astype(bf16))

    def remote(source, target, phase, slot, peer):
        copy = pltpu.make_async_remote_copy(
            src_ref=source, dst_ref=target, send_sem=block_send.at[phase, slot], recv_sem=block_recv.at[phase, slot],
            device_id=(seg, peer), device_id_type=MESH)
        copy.start()
        pending.append(copy)
        return copy

    def rows_of(k, column):
        return pl.ds(pl.multiple_of((row_order[k] * SIDE + column) * rows, rows), rows)

    def image(source, vector, sent, side, phase, scale, first, more):
        lanes = slice(first, 1024)
        dots = jnp.zeros((8, 128), f32)
        copies = []
        for k in range(ROW):
            span = pl.ds(pl.multiple_of(row_order[k] * 256, 256), 256)
            if not more:
                couple(row_order[k], source)
            part = jnp.dot(source[span, lanes], stacked[lanes, :], preferred_element_type=f32)
            if more:
                part = part + partial[span, :]
            dots = dots + jnp.sum((part * vector[span, :].astype(f32)).reshape(32, 8, 128), axis=0)
            if scale is not None:
                part = part * scale
            partial[span, :] = part
            sent[span, :] = part.astype(bf16)
            for j in (2, 1, 3):
                column = lax.rem(place + j, SIDE)
                slot = k * 3 + j - 1
                copies.append(remote(
                    sent.at[rows_of(k, column), :], side.at[slot], phase, slot, row * SIDE + column))
        return total(dots), copies

    def along_z(phase, copies, side, sent, target):
        onward = []
        for k in range(ROW):
            value = partial[rows_of(k, place), :]
            for copy in copies[3 * k:3 * k + 3]:
                copy.wait_recv()
            for slot in range(3 * k, 3 * k + 3):
                value = value + side[slot].astype(f32)
            if k < 3:
                sent[k] = value.astype(bf16)
                onward.append(remote(sent.at[k], target.at[k], phase, 12 + k, row_order[k] * SIDE + place))
        return value, onward

    def scatter_sum(value, onward, target):
        for k in (2, 1, 0):
            onward[k].wait_recv()
            value = value + target[k].astype(f32)
        return value

    def grow(pairs, target):
        for u in range(0, 8, 2):
            lanes = slice(u * 128, (u + 2) * 128)
            value = None
            for transposed, source in pairs:
                term = jnp.dot(transposed[...], source[:, lanes], preferred_element_type=f32)
                value = term if value is None else value + term
            target[pl.ds(u, 128, stride=8), :] = value[:, :128]
            target[pl.ds(u + 1, 128, stride=8), :] = value[:, 128:]

    def scalar_round(phase, value):
        scal_send[phase] = jnp.broadcast_to(value, (1, 128))
        copies = []
        for step, peer in enumerate(peers):
            copies.append(pltpu.make_async_remote_copy(
                src_ref=scal_send.at[phase], dst_ref=scal_recv.at[phase, me],
                send_sem=scal_send_sem.at[phase, step], recv_sem=scal_recv_sem.at[phase, step],
                device_id=(seg, peer), device_id_type=MESH))
            copies[-1].start()
        scal_recv[phase, me] = scal_send[phase]
        return copies

    def scalar_sum(phase, copies):
        for copy in copies:
            copy.wait()
        return jnp.sum(scal_recv[phase], axis=0)[:, :1]

    own = pl.ds(pl.multiple_of(me * rows, rows), rows)

    loads[1].wait()
    spread[...] = start[...].astype(f32)
    for t in range(8):
        wide[:, t * 128:(t + 1) * 128] = spread[pl.ds(t, 128, stride=8), :].astype(bf16)
    norm = total(jnp.sum((spread[...] * spread[...]).reshape(-1, 8, 128), axis=0))
    inverse = 1.0 / jnp.sqrt(norm / entries + epsilon)
    loads[3].wait()
    spot = lax.broadcasted_iota(jnp.int32, (8, 256), 0)
    wide_lane = lax.broadcasted_iota(jnp.int32, (8, 256), 1)
    compact = jnp.zeros((64, 256), f32)
    for w in range(8):
        chosen = jnp.where(lax.rem(wide_lane, 64) == spot * 8 + w, 1.0, 0.0).astype(f32)
        compact = compact + jnp.dot(
            mpo[w].astype(f32).reshape(64, 8), chosen, preferred_element_type=f32)
    tall = jnp.concatenate([compact] * 4, axis=0)
    row_group = lax.broadcasted_iota(jnp.int32, (256, 256), 0) // 64
    lane_group = lax.broadcasted_iota(jnp.int32, (256, 256), 1) // 64
    coupler[...] = jnp.where(row_group == lane_group, tall, 0.0).astype(bf16)
    loads[2].wait()
    for i in range(ROW):
        couple(i, coupled_1)
    start_t[...] = jnp.transpose(start[...])

    ring[0].wait_recv()
    for c in range(CHUNKS):
        ring[1 + c].wait_recv()
        for u in range(c * share, (c + 1) * share):
            unpack(u)
        if c < CHUNKS - 1:
            def add(i, carry, c=c):
                span, lanes = pl.ds(i * 256, 256), slice(c * share * 128, (c + 1) * share * 128)
                part = jnp.dot(coupled_1[span, lanes], stacked[lanes, :], preferred_element_type=f32)
                partial[span, :] = part if c == 0 else partial[span, :] + part
                return carry
            lax.fori_loop(0, 4, add, 0)
    pl.when(me < bonds - 1)(lambda: pl.semaphore_wait(ready, bonds - 1 - me))
    ray, copies = image(coupled_1, start, send_1, side_1, 0, None, (CHUNKS - 1) * share * 128, True)
    ray_copies = scalar_round(0, ray)
    grow([(start_t, coupled_1)], grown_11)
    @pl.when(early)
    def _():
        pl.semaphore_wait(distant, 1)
        for copy in ring:
            copy.start()

    value, onward = along_z(0, copies, side_1, sums_1, recv_1)
    rayleigh = scalar_sum(0, ray_copies) * (inverse * inverse / entries)
    image_1 = scatter_sum(value, onward, recv_1)
    block = inverse * image_1 - (rayleigh * inverse) * start[own, :].astype(f32)
    resid[own, :] = block.astype(bf16)

    def spread_out(k):
        held = resid.at[rows_of(k, place), :]
        return [remote(held, held, 1, k * 3 + j - 1, row * SIDE + lax.rem(place + j, SIDE)) for j in (2, 1, 3)]

    mine = resid.at[own, :]
    onward = [remote(mine, mine, 1, 12 + k, row_order[k] * SIDE + place) for k in range(3)]
    relayed = {3: spread_out(3)}
    size_copies = scalar_round(1, total(block * block))
    for k in (2, 1, 0):
        onward[k].wait_recv()
        relayed[k] = spread_out(k)

    for k in (3, 2, 1, 0):
        for copy in relayed[k]:
            copy.wait_recv()
        span = pl.ds(pl.multiple_of(row_order[k] * 256, 256), 256)
        spread[span, :] = resid[span, :].astype(f32)
        for t in range(8):
            wide[pl.ds(pl.multiple_of(row_order[k] * 32, 32), 32), t * 128:(t + 1) * 128] = (
                spread[pl.ds(row_order[k] * 256 + t, 32, stride=8), :].astype(bf16))

    size = jnp.sqrt(scalar_sum(1, size_copies) / entries + epsilon)
    curve, copies = image(coupled_2, resid, send_2, side_2, 2, 1.0 / size, 0, False)
    curve_copies = scalar_round(2, curve)
    resid_t[...] = jnp.transpose(resid[...])
    grow([(start_t, coupled_2), (resid_t, coupled_1)], grown_x)
    value, onward = along_z(2, copies, side_2, sums_2, recv_2)
    grow([(resid_t, coupled_2)], grown_22)
    curvature = scalar_sum(2, curve_copies) / (size * size * entries)
    middle = 0.5 * (rayleigh + curvature)
    half_gap = 0.5 * (rayleigh - curvature)
    lowest = middle - jnp.sqrt(half_gap * half_gap + size * size)
    offset = lowest - rayleigh
    length = jnp.sqrt(size * size + offset * offset)
    first = size / length * inverse
    second = offset / length / size
    energy_ref[...] = jnp.broadcast_to(lowest, (8, 128))
    state_ref[...] = (first * start[...].astype(f32) + second * resid[...].astype(f32)).astype(bf16)
    grown_ref[...] = (first * first * grown_11[...] + first * second * grown_x[...]
                      + second * second * grown_22[...]).astype(bf16)
    for copy in ring + pending:
        copy.wait_send()
    image_ref[...] = scatter_sum(value, onward, recv_2)


def write_out(state, grown, energy, image, state_out, grown_out, energy_out, image_out, lowest, sems):
    copies = [
        pltpu.make_async_copy(source, target, sems.at[spot])
        for spot, (source, target) in enumerate(((state, state_out), (grown, grown_out), (image, image_out)))
    ]
    for copy in copies:
        copy.start()
    lowest[0] = energy[0, 0]
    copies.append(pltpu.make_async_copy(lowest, energy_out, sems.at[3]))
    copies[3].start()
    for copy in copies:
        copy.wait()


def solution(mesh):
    segs, bonds = mesh.shape["seg"], mesh.shape["bond"]

    def body(left_env, right_env, mpo_site, start_state):
        big, half = (1024, 128), (1024 // bonds, 128)
        anywhere = pl.BlockSpec(memory_space=pl.ANY)
        vmem = pl.BlockSpec(memory_space=pltpu.VMEM)
        results = pl.pallas_call(
            lambda *refs: kernel(segs, bonds, *refs),
            out_shape=(pltpu.VMEM(big, bf16), pltpu.VMEM(big, bf16), pltpu.VMEM((8, 128), f32), pltpu.VMEM(half, f32)),
            in_specs=[pl.BlockSpec(memory_space=pltpu.HBM)] * 4,
            out_specs=(vmem,) * 4,
            scratch_shapes=[
                pltpu.VMEM(big, bf16),
                pltpu.VMEM(big, bf16),
                pltpu.VMEM((8, 8, 8, 8), bf16),
                pltpu.VMEM(big, bf16),
                pltpu.VMEM(big, f32),
                pltpu.VMEM((128, 1024), bf16),
                pltpu.VMEM(big, bf16),
                pltpu.VMEM((256, 256), bf16),
                pltpu.VMEM((8, 64, 128), bf16),
                pltpu.VMEM((8, 64, 128), bf16),
                pltpu.VMEM((8, 128), f32),
                pltpu.VMEM((8, 128), f32),
                pltpu.VMEM((1024, 1024), bf16),
                pltpu.VMEM((1024, 1024), bf16),
                pltpu.VMEM(big, f32),
                pltpu.VMEM((128, 1024), bf16),
                pltpu.VMEM((128, 1024), bf16),
                pltpu.VMEM(big, bf16),
                pltpu.VMEM(big, bf16),
                pltpu.VMEM((12,) + half, bf16),
                pltpu.VMEM((12,) + half, bf16),
                pltpu.VMEM((3,) + half, bf16),
                pltpu.VMEM((3,) + half, bf16),
                pltpu.VMEM((3,) + half, bf16),
                pltpu.VMEM((3,) + half, bf16),
                pltpu.VMEM(big, bf16),
                pltpu.VMEM((3, 1, 128), f32),
                pltpu.VMEM((3, bonds, 1, 128), f32),
                pltpu.VMEM(big, f32),
                pltpu.VMEM(big, f32),
                pltpu.VMEM(big, f32),
                pltpu.SemaphoreType.REGULAR,
                pltpu.SemaphoreType.REGULAR,
                pltpu.SemaphoreType.DMA((4,)),
                pltpu.SemaphoreType.DMA((CHUNKS + 1,)),
                pltpu.SemaphoreType.DMA((CHUNKS + 1,)),
                pltpu.SemaphoreType.DMA((3, bonds - 1)),
                pltpu.SemaphoreType.DMA((3, bonds - 1)),
                pltpu.SemaphoreType.DMA((3, bonds - 1)),
                pltpu.SemaphoreType.DMA((3, bonds - 1)),
            ],
            compiler_params=pltpu.CompilerParams(
                collective_id=0, has_side_effects=True, vmem_limit_bytes=32 * 1024 * 1024),
            name="ritz_step",
        )(*(pltpu.with_memory_space_constraint(x, pltpu.HBM) for x in (
            left_env.reshape(big), right_env.reshape(big), mpo_site[0], start_state.reshape(big))))
        state, grown, energy, image = pl.pallas_call(
            write_out,
            out_shape=(
                jax.ShapeDtypeStruct(big, bf16),
                jax.ShapeDtypeStruct(big, bf16),
                jax.ShapeDtypeStruct((1,), f32),
                jax.ShapeDtypeStruct(half, f32),
            ),
            in_specs=[vmem] * 4,
            out_specs=(anywhere,) * 4,
            scratch_shapes=[pltpu.SMEM((1,), f32), pltpu.SemaphoreType.DMA((4,))],
            compiler_params=pltpu.CompilerParams(vmem_limit_bytes=8 * 1024 * 1024),
            name="write_out",
        )(*results)
        return (
            state.reshape(1, 128, 8, 128),
            grown.reshape(1, 128, 8, 128),
            energy,
            image.reshape(1, 1024 // bonds // 8, 8, 128),
        )

    in_specs = (
        P("seg", None, "bond", None),
        P("seg", None, "bond", None),
        P("seg", "bond", None, None, None),
        P("seg", None, None, None),
    )
    out_specs = (
        P("seg", None, None, None),
        P("seg", None, "bond", None),
        P("seg"),
        P("seg", "bond", None, None),
    )
    return jax.shard_map(body, mesh=mesh, in_specs=in_specs, out_specs=out_specs, check_vma=False)
```
